32 devices in a mesh: paths: 2 (over x), hi: 16 (over z, y, core).
Axes of the slice: x: 2, y: 2, z: 4, core: 2. Of those that a mesh axis runs over, the one named last changes fastest.
Arguments:
- amplitudes: float32 [2, 2097152], P(None, ('paths', 'hi')), parts along dimension 1, may hold values from -6 to 6
- gate_matrices: bfloat16 [6, 2, 128, 128], replicated, may hold values from -0.375 to 0.375
- phase_qubits: int32 [12, 8, 2], P('paths'), parts along dimension 0, may hold values from 0 to 19
- phase_angles: float32 [12, 8], P('paths'), parts along dimension 0, may hold values from -3.140625 to 3.140625
- cut_qubits: int32 [12, 2], P('paths'), parts along dimension 0, may hold values from 0 to 19
- cut_angle: float32 [12], P('paths'), parts along dimension 0, may hold values from 0.6 to 0.97
- path_index: int32 [12], P('paths'), parts along dimension 0, may hold values from 0 to 1
Outputs:
- final_state: float32 [2, 2097152], P(None, ('paths', 'hi')), parts along dimension 1
The draws below stay inside these ranges and needn't reach their ends.
There are 2 independent parts, one for each index of `paths`. The reference program is written for one: setup_inputs(seed, part) draws one part's arguments, and reference() takes and returns one part's arrays. A program takes and returns all parts, laid end to end along the dimension named above; an argument that names none is the same for every part. Nothing has to cross between parts.
All inputs are finite; a program needn't handle non-finite values.
Results may differ from the reference program's by a relative error of at most 0.0003.
Values sent between devices are 32-bit elements; how exact they have to be, the bound alone decides.
A program may use at most 64 MiB of HBM per device.

```python
import jax
import jax.numpy as jnp
from jax import lax

LOCAL_Q = 16
GLOBAL_Q = 4
QUBITS = 20
AMPS = 1048576
GATE_DIM = 128
LAYERS = 6
PAIRS = 8
CUTS = 6


def set_ends(entries, key, least, top_value):
    dims = entries.shape
    index_at = [jax.random.randint(jax.random.fold_in(key, axis), (), 0, dims[axis]) for axis in range(len(dims))]
    entries = entries.at[tuple(index_at)].set(least)
    longest = dims.index(max(dims))
    index_at[longest] = (index_at[longest] + 1) % dims[longest]
    return entries.at[tuple(index_at)].set(top_value)


def levels(key, extent, cuts, low, high):
    def one(position, parts):
        heights = jax.random.uniform(jax.random.fold_in(jax.random.fold_in(key, 6), position), (parts,), jnp.float32, low / len(cuts), high / len(cuts))
        return jnp.repeat(jnp.exp(heights), extent[position] // parts).reshape((-1,) + (1,) * (len(extent) - position - 1))

    level = one(*cuts[0])
    for cut in cuts[1:]:
        level = level * one(*cut)
    return level


def centred(rng, shape, deviation, bound, cuts=(), held_as=jnp.bfloat16):
    drawn = jax.random.normal(rng, shape, jnp.float32) * deviation
    if len(cuts) > 0:
        drawn = levels(rng, shape, cuts, -0.22, 0.18) * drawn
    return jnp.clip(drawn, min=-bound, max=bound).astype(held_as)


def setup_inputs(seed: int = 0, part: int = 0) -> dict:
    keys = jax.random.split(jax.random.key(seed), 8)
    part_keys = jax.random.split(jax.random.fold_in(keys[7], part), 8)
    return {
        "amplitudes": centred(part_keys[0], (2, AMPS), 1.0, 6.0, ((1, 16),), jnp.float32),
        "gate_matrices": centred(keys[1], (LAYERS, 2, GATE_DIM, GATE_DIM), (2 * GATE_DIM) ** -0.5, 0.375),
        "phase_qubits": set_ends(jax.random.randint(part_keys[2], (LAYERS, PAIRS, 2), 0, QUBITS), jax.random.fold_in(part_keys[2], 1), 0, QUBITS - 1).astype(jnp.int32),
        "phase_angles": jnp.clip(jax.random.uniform(part_keys[3], (LAYERS, PAIRS), jnp.float32, -3.140625, 3.140625), -3.140625, 3.140625),
        "cut_qubits": set_ends(jax.random.randint(part_keys[4], (CUTS, 2), 0, QUBITS), jax.random.fold_in(part_keys[4], 1), 0, QUBITS - 1).astype(jnp.int32),
        "cut_angle": jnp.clip(jax.random.uniform(part_keys[5], (CUTS,), jnp.float32, 0.6, 0.97), 0.6, 0.97),
        "path_index": set_ends(jax.random.randint(part_keys[6], (CUTS,), 0, 2), jax.random.fold_in(part_keys[6], 1), 0, 1).astype(jnp.int32),
    }


def real_form(matrix):
    real_part = matrix[0].astype(jnp.float32)
    imag_part = matrix[1].astype(jnp.float32)
    upper_rows = jnp.stack((real_part, -imag_part), axis=1)
    lower_rows = jnp.stack((imag_part, real_part), axis=1)
    stacked = jnp.stack((upper_rows, lower_rows), axis=0)
    return stacked.reshape(2, 2, 64, 2, 2, 64)


def apply_gate(amps_now, matrix, target, total_bits):
    shaped = amps_now.reshape(2, 2 ** (total_bits - 1 - target), 2, 2 ** (target - 7), 2, 64)
    result = jnp.einsum("wxyzbd,zabced->waxcey", real_form(matrix), shaped,
                        precision=lax.Precision.HIGHEST)
    return result.reshape(2, -1)


def swap_bits(amps_now, low_bit, high_bit, total_bits):
    shaped = amps_now.reshape(2, 2 ** (total_bits - 1 - high_bit), 2, 2 ** (high_bit - low_bit - 1), 2, 2 ** low_bit)
    return jnp.swapaxes(shaped, 2, 4).reshape(2, -1)


def rotate(amps_now, theta):
    cosine = jnp.cos(theta)
    sine = jnp.sin(theta)
    return jnp.stack((cosine * amps_now[0] - sine * amps_now[1], sine * amps_now[0] + cosine * amps_now[1]))


def bit_of(index_all, qubit):
    return jnp.bitwise_and(jnp.right_shift(index_all, qubit), 1)


def reference(amplitudes, gate_matrices, phase_qubits, phase_angles, cut_qubits, cut_angle, path_index):
    total_bits = QUBITS
    index_all = lax.iota(jnp.int32, 2 ** total_bits)
    result = amplitudes
    for layer_number in range(LAYERS):
        if layer_number < GLOBAL_Q:
            result = swap_bits(result, 7 + layer_number, LOCAL_Q + layer_number, total_bits)
            target = 7 + layer_number
        else:
            if layer_number == GLOBAL_Q:
                block_size = 2 ** GLOBAL_Q
                shaped = result.reshape(2, block_size, block_size, 2 ** (LOCAL_Q - GLOBAL_Q))
                result = jnp.swapaxes(shaped, 1, 2).reshape(2, -1)
            target = LOCAL_Q - 2 * GLOBAL_Q + layer_number
        result = apply_gate(result, gate_matrices[layer_number], target, total_bits)
        theta = jnp.zeros((2 ** total_bits,), jnp.float32)
        for pair_number in range(PAIRS):
            first_bit = bit_of(index_all, phase_qubits[layer_number, pair_number, 0])
            second_bit = bit_of(index_all, phase_qubits[layer_number, pair_number, 1])
            theta = theta + phase_angles[layer_number, pair_number] * (first_bit * second_bit).astype(jnp.float32)
        result = rotate(result, theta)
        if layer_number == 0:
            for cut_number in range(CUTS):
                parity = jnp.bitwise_xor(bit_of(index_all, cut_qubits[cut_number, 0]), bit_of(index_all, cut_qubits[cut_number, 1]))
                signs = (1 - 2 * parity).astype(jnp.float32)
                chosen = path_index[cut_number] == 0
                angle_now = cut_angle[cut_number]
                keep_part = jnp.where(chosen, jnp.cos(angle_now), jnp.zeros_like(angle_now))
                turn_part = jnp.where(chosen, jnp.zeros_like(angle_now), jnp.sin(angle_now))
                result = jnp.stack((keep_part * result[0] + turn_part * signs * result[1],
                                    keep_part * result[1] - turn_part * signs * result[0]))
    return result
```

```python
import functools
import math

import jax
import jax.numpy as jnp
from jax import lax
from jax.experimental import pallas as pl
from jax.experimental.pallas import tpu as pltpu
from jax.sharding import PartitionSpec as P

LANES = 128
SUB = 8
MESH = pl.DeviceIdType.MESH


def quarter_sincos(turns):
    whole = jnp.floor(turns + 0.5)
    rest = turns - whole
    square = rest * rest
    half_pi = math.pi / 2
    sin_terms = [(-1) ** k * half_pi ** (2 * k + 1) / math.factorial(2 * k + 1) for k in range(5)]
    cos_terms = [(-1) ** k * half_pi ** (2 * k) / math.factorial(2 * k) for k in range(6)]
    sine = jnp.full_like(square, sin_terms[-1])
    for term in sin_terms[-2::-1]:
        sine = sine * square + term
    sine = sine * rest
    cosine = jnp.full_like(square, cos_terms[-1])
    for term in cos_terms[-2::-1]:
        cosine = cosine * square + term
    count = whole.astype(jnp.int32)
    odd = (count & 1) == 1
    sin_out = jnp.where(odd, cosine, sine)
    cos_out = jnp.where(odd, sine, cosine)
    sin_out = jnp.where((count & 2) == 2, -sin_out, sin_out)
    cos_out = jnp.where(((count + 1) & 2) == 2, -cos_out, cos_out)
    return sin_out, cos_out


def swap_half(value):
    return pltpu.roll(value, LANES // 2, axis=1)


def spread(value, moves):
    total = None
    for a, b in moves:
        term = ((value >> a) & 1) << b
        total = term if total is None else total + term
    return total


def circuit_kernel(
    g, local_bits, layers, pairs, cuts,
    amp_ref, gate_ref, qubit_ref, angle_ref, cut_qubit_ref, cut_angle_ref, path_ref,
    out_ref, recv, weights, gates, cos_all, sin_all, turned,
    send_sem, recv_sem, own_sem, gate_sem,
):
    n = 2**g
    block_bits = local_bits - g - 7
    chunks = 2 ** (block_bits - 3)
    piece = 2 * SUB
    rows = n * SUB
    me = lax.axis_index("hi")
    order = sorted(range(1, n), key=lambda off: abs(off - n // 2))

    def block_rows(owner, chunk):
        return pl.ds(pl.multiple_of((owner * chunks + chunk) * piece, piece), piece)

    def slot_rows(source):
        return pl.ds(pl.multiple_of(source * piece, piece), piece)

    def remote(chunk, off):
        peer = lax.rem(me + off, n)
        return pltpu.make_async_remote_copy(
            src_ref=amp_ref.at[block_rows(peer, chunk)],
            dst_ref=recv.at[chunk, slot_rows(me)],
            send_sem=send_sem.at[chunk, off],
            recv_sem=recv_sem.at[chunk, off],
            device_id={"hi": peer},
            device_id_type=MESH,
        )

    def own(chunk):
        return pltpu.make_async_copy(
            amp_ref.at[block_rows(me, chunk)], recv.at[chunk, slot_rows(me)], own_sem.at[chunk]
        )

    gate_copy = pltpu.make_async_copy(gate_ref, gates, gate_sem)
    gate_copy.start()

    barrier = pltpu.get_barrier_semaphore()
    for off in order:
        pl.semaphore_signal(
            barrier, inc=1, device_id={"hi": lax.rem(me + off, n)}, device_id_type=MESH
        )
    pl.semaphore_wait(barrier, n - 1)

    @pl.loop(0, chunks)
    def _(chunk):
        for off in order:
            remote(chunk, off).start()
        own(chunk).start()

    gate_copy.wait()
    low_lanes = lax.broadcasted_iota(jnp.int32, (64, LANES), 1) < 64

    @pl.loop(0, layers)
    def _(layer):
        real_t = gates[layer, 0].astype(jnp.float32).T
        imag_t = gates[layer, 1].astype(jnp.float32).T
        for t in range(2):
            real_rows = real_t[t * 64 : (t + 1) * 64]
            imag_rows = imag_t[t * 64 : (t + 1) * 64]
            real_turned, imag_turned = swap_half(real_rows), swap_half(imag_rows)
            parts = (
                (
                    jnp.where(low_lanes, real_rows, imag_turned),
                    jnp.where(low_lanes, real_turned, imag_rows),
                ),
                (
                    jnp.where(low_lanes, -imag_rows, real_turned),
                    jnp.where(low_lanes, -imag_turned, real_rows),
                ),
            )
            for c in range(2):
                for t_out in range(2):
                    weights[
                        layer,
                        t * 128 + c * 64 : t * 128 + c * 64 + 64,
                        t_out * 128 : t_out * 128 + 128,
                    ] = parts[c][t_out].astype(jnp.bfloat16)

    def chunk_row(k):
        return block_bits + 3 + k if 10 + k < 7 + g else 3 + k

    lane = lax.broadcasted_iota(jnp.int32, (n, SUB, LANES), 2)
    first = lax.broadcasted_iota(jnp.int32, (n, SUB, LANES), 0)
    second = lax.broadcasted_iota(jnp.int32, (n, SUB, LANES), 1)
    flat_low = lax.broadcasted_iota(jnp.int32, (rows, LANES), 1) < 64
    to_quarter = 2.0 / math.pi

    def entry_index(layer, chunk):
        def place(q):
            if 7 <= q <= 7 + layer:
                return q - 7 + local_bits
            if local_bits <= q <= local_bits + layer:
                return q - local_bits + 7
            return q

        scalar = spread(chunk, [(k, place(10 + k)) for k in range(block_bits - 3)]) + spread(
            me, [(k, place(local_bits - g + k)) for k in range(g)]
        )
        return (
            (lane + spread(second, [(k, place(7 + k)) for k in range(3)]) + scalar)
            + spread(first, [(k, place(local_bits + k)) for k in range(g)])
        )

    def final_index(chunk):
        low_part = lax.broadcasted_iota(jnp.int32, (SUB, n, LANES), 0)
        source = lax.broadcasted_iota(jnp.int32, (SUB, n, LANES), 1)
        lane_part = lax.broadcasted_iota(jnp.int32, (SUB, n, LANES), 2)
        scalar = spread(chunk, [(k, 7 + chunk_row(k)) for k in range(block_bits - 3)])
        return lane_part + (source << 7) + (low_part << (7 + block_bits)) + (
            scalar + (me << local_bits)
        )

    cut_mask = jnp.int32(0)
    cut_turns = jnp.float32(0)
    cut_size = jnp.full((SUB, LANES), 1.0, jnp.float32)
    for k in range(cuts):
        kept = path_ref[k] == 0
        bits = (jnp.int32(1) << cut_qubit_ref[k, 0]) ^ (jnp.int32(1) << cut_qubit_ref[k, 1])
        cut_mask = cut_mask ^ jnp.where(kept, 0, bits)
        cut_turns = cut_turns - jnp.where(kept, 0.0, 1.0)
        sine, cosine = quarter_sincos(
            jnp.full((SUB, LANES), cut_angle_ref[k], jnp.float32) * to_quarter
        )
        kept_all = jnp.full((SUB, LANES), path_ref[k], jnp.int32) == 0
        cut_size = cut_size * jnp.where(kept_all, cosine, sine)

    for layer in range(layers):
        masks = []
        for k in range(pairs):
            mask = (jnp.int32(1) << qubit_ref[layer, k, 0]) | (
                jnp.int32(1) << qubit_ref[layer, k, 1]
            )
            masks.append((mask, angle_ref[layer, k] * to_quarter))

        @pl.loop(0, chunks)
        def _(chunk):
            index = entry_index(layer, chunk) if layer < g else final_index(chunk)
            index = index.reshape(rows, LANES)
            turns = jnp.zeros((rows, LANES), jnp.float32)
            for mask, angle in masks:
                turns = turns + jnp.where((index & mask) == mask, angle, 0.0)
            if layer == 0:
                folded = index & cut_mask
                for shift in (16, 8, 4, 2, 1):
                    folded = folded ^ (folded >> shift)
                turns = turns + cut_turns + ((folded & 1) * 2).astype(jnp.float32)
            sine, cosine = quarter_sincos(turns)
            if layer == 0:
                size = jnp.broadcast_to(cut_size[None], (n, SUB, LANES)).reshape(rows, LANES)
                sine, cosine = sine * size, cosine * size
            sine_turned, cosine_turned = swap_half(sine), swap_half(cosine)
            cos_all[layer, chunk, 0] = jnp.where(flat_low, cosine, cosine_turned)
            cos_all[layer, chunk, 1] = jnp.where(flat_low, cosine_turned, cosine)
            sin_all[layer, chunk, 0] = jnp.where(flat_low, -sine, sine_turned)
            sin_all[layer, chunk, 1] = jnp.where(flat_low, -sine_turned, sine)

    def layer_step(state, layer, chunk, outer, inner):
        shaped = state.reshape(2, outer, 2, inner, LANES)
        joined = jnp.concatenate(
            (shaped[:, :, 0].reshape(rows, LANES), shaped[:, :, 1].reshape(rows, LANES)), axis=1
        )
        high = joined.astype(jnp.bfloat16)
        rest = (joined - high.astype(jnp.float32)).astype(jnp.bfloat16)
        gate = weights[layer]
        product = jnp.dot(high, gate, preferred_element_type=jnp.float32) + jnp.dot(
            rest, gate, preferred_element_type=jnp.float32
        )
        back = jnp.stack(
            (
                product[:, :LANES].reshape(2, outer, inner, LANES),
                product[:, LANES:].reshape(2, outer, inner, LANES),
            ),
            axis=2,
        ).reshape(2 * rows, LANES)
        cosine = cos_all[layer, chunk].reshape(2 * rows, LANES)
        sine = sin_all[layer, chunk].reshape(2 * rows, LANES)
        return back * cosine + swap_half(back) * sine

    @pl.loop(0, chunks)
    def _(chunk):
        own(chunk).wait()
        for off in order:
            remote(chunk, off).wait_recv()
        real = recv[chunk, pl.ds(0, rows, stride=2), :]
        imag = recv[chunk, pl.ds(1, rows, stride=2), :]
        state = jnp.concatenate(
            (
                jnp.where(flat_low, real, swap_half(imag)),
                jnp.where(flat_low, swap_half(real), imag),
            ),
            axis=0,
        )
        for layer in range(g):
            state = layer_step(state, layer, chunk, 2 ** (g - 1 - layer), 2**layer * SUB)
        turned[...] = state
        state = jnp.concatenate(
            [
                turned[pl.ds(b * rows + low, n, stride=SUB), :]
                for b in range(2)
                for low in range(SUB)
            ],
            axis=0,
        )
        for layer in range(g, layers):
            k = layer - g
            state = layer_step(state, layer, chunk, 2 ** (2 - k), 2**k * n)
        zero, one = state[:rows], state[rows:]
        real = jnp.where(flat_low, zero, swap_half(one))
        imag = jnp.where(flat_low, swap_half(zero), one)
        base = spread(chunk, [(k, chunk_row(k)) for k in range(block_bits - 3)])
        for low in range(SUB):
            start = pl.multiple_of(2 * (base + (low << block_bits)), 2 * n)
            out_ref[pl.ds(start, n, stride=2), :] = real[low * n : (low + 1) * n]
            out_ref[pl.ds(start + 1, n, stride=2), :] = imag[low * n : (low + 1) * n]

    @pl.loop(0, chunks)
    def _(chunk):
        for off in order:
            remote(chunk, off).wait_send()


def one_exchange(
    amplitudes, gate_matrices, phase_qubits, phase_angles, cut_qubits, cut_angle, path_index
):
    g = lax.axis_size("hi").bit_length() - 1
    amp_count = amplitudes.shape[1]
    local_bits = amp_count.bit_length() - 1
    layers, pairs = phase_angles.shape
    cuts = cut_angle.shape[0]
    n = 2**g
    chunks = 2 ** (local_bits - g - 10)
    rows = n * SUB
    all_rows = amp_count // LANES
    whole = amplitudes.reshape(2, all_rows, LANES).transpose(1, 0, 2).reshape(2 * all_rows, LANES)
    smem = pl.BlockSpec(memory_space=pltpu.SMEM)
    hbm = pl.BlockSpec(memory_space=pl.ANY)
    result = pl.pallas_call(
        functools.partial(circuit_kernel, g, local_bits, layers, pairs, cuts),
        out_shape=jax.ShapeDtypeStruct((2 * all_rows, LANES), jnp.float32),
        in_specs=[hbm, hbm, smem, smem, smem, smem, smem],
        out_specs=pl.BlockSpec(memory_space=pltpu.VMEM),
        scratch_shapes=[
            pltpu.VMEM((chunks, 2 * rows, LANES), jnp.float32),
            pltpu.VMEM((layers, 256, 256), jnp.bfloat16),
            pltpu.VMEM(gate_matrices.shape, jnp.bfloat16),
            pltpu.VMEM((layers, chunks, 2, rows, LANES), jnp.float32),
            pltpu.VMEM((layers, chunks, 2, rows, LANES), jnp.float32),
            pltpu.VMEM((2 * rows, LANES), jnp.float32),
            pltpu.SemaphoreType.DMA((chunks, n)),
            pltpu.SemaphoreType.DMA((chunks, n)),
            pltpu.SemaphoreType.DMA((chunks,)),
            pltpu.SemaphoreType.DMA,
        ],
        compiler_params=pltpu.CompilerParams(collective_id=0, has_side_effects=True),
    )(whole, gate_matrices, phase_qubits, phase_angles, cut_qubits, cut_angle, path_index)
    return result.reshape(all_rows, 2, LANES).transpose(1, 0, 2).reshape(2, amp_count)


def from_partner(value, axis, bit):
    return lax.ppermute(value, axis, [(i, i ^ 1 << bit) for i in range(lax.axis_size(axis))])


def real_form(matrix):
    real_part = matrix[0].astype(jnp.float32)
    imag_part = matrix[1].astype(jnp.float32)
    upper_rows = jnp.stack((real_part, -imag_part), axis=1)
    lower_rows = jnp.stack((imag_part, real_part), axis=1)
    stacked = jnp.stack((upper_rows, lower_rows), axis=0)
    return stacked.reshape(2, 2, 64, 2, 2, 64)


def apply_gate(amps_now, matrix, target, local_bits):
    shaped = amps_now.reshape(2, 2 ** (local_bits - 1 - target), 2, 2 ** (target - 7), 2, 64)
    result = jnp.einsum(
        "wxyzbd,zabced->waxcey", real_form(matrix), shaped, precision=lax.Precision.HIGHEST
    )
    return result.reshape(2, -1)


def rotate(amps_now, theta):
    cosine = jnp.cos(theta)
    sine = jnp.sin(theta)
    return jnp.stack(
        (cosine * amps_now[0] - sine * amps_now[1], sine * amps_now[0] + cosine * amps_now[1])
    )


def bit_of(index_all, qubit):
    return jnp.bitwise_and(jnp.right_shift(index_all, qubit), 1)


def located(qubit, first_open, global_count, local_bits):
    moved_up = (qubit >= 7 + first_open) & (qubit < 7 + global_count)
    moved_down = (qubit >= local_bits + first_open) & (qubit < local_bits + global_count)
    return jnp.where(
        moved_up, qubit - 7 + local_bits, jnp.where(moved_down, qubit - local_bits + 7, qubit)
    )


def enter_qubit(amps_now, bit_number, local_bits, device_place):
    shaped = amps_now.reshape(2, 2 ** (local_bits - 8 - bit_number), 2, 2**bit_number, 128)
    zero_half = shaped[:, :, 0]
    one_half = shaped[:, :, 1]
    upper_side = jnp.bitwise_and(jnp.right_shift(device_place, bit_number), 1) == 1
    kept_half = jnp.where(upper_side, one_half, zero_half)
    sent_half = jnp.where(upper_side, zero_half, one_half)
    came_half = from_partner(sent_half, "hi", bit_number)
    new_zero = jnp.where(upper_side, came_half, kept_half)
    new_one = jnp.where(upper_side, kept_half, came_half)
    return jnp.stack((new_zero, new_one), axis=2).reshape(2, -1)


def shards(
    amplitudes, gate_matrices, phase_qubits, phase_angles, cut_qubits, cut_angle, path_index
):
    global_count = lax.axis_size("hi").bit_length() - 1
    amp_count = amplitudes.shape[1]
    local_bits = amp_count.bit_length() - 1
    device_place = lax.axis_index("hi")
    index_all = device_place * amp_count + lax.iota(jnp.int32, amp_count)
    layer_count = gate_matrices.shape[0]
    result = amplitudes
    for layer_number in range(layer_count):
        if layer_number < global_count:
            result = enter_qubit(result, layer_number, local_bits, device_place)
            target = 7 + layer_number
        else:
            if layer_number == global_count:
                shaped = result.reshape(2, 2**global_count, 2 ** (local_bits - global_count))
                result = lax.all_to_all(
                    shaped, "hi", split_axis=1, concat_axis=1, tiled=True
                ).reshape(2, -1)
            target = local_bits - 2 * global_count + layer_number
        result = apply_gate(result, gate_matrices[layer_number], target, local_bits)
        theta = jnp.zeros((amp_count,), jnp.float32)
        for pair_number in range(phase_qubits.shape[1]):
            first_pos = located(
                phase_qubits[layer_number, pair_number, 0], global_count, global_count, local_bits
            )
            second_pos = located(
                phase_qubits[layer_number, pair_number, 1], global_count, global_count, local_bits
            )
            both_bits = bit_of(index_all, first_pos) * bit_of(index_all, second_pos)
            theta = theta + phase_angles[layer_number, pair_number] * both_bits.astype(jnp.float32)
        result = rotate(result, theta)
        if layer_number == 0:
            for cut_number in range(cut_qubits.shape[0]):
                first_cut = located(
                    cut_qubits[cut_number, 0], global_count, global_count, local_bits
                )
                second_cut = located(
                    cut_qubits[cut_number, 1], global_count, global_count, local_bits
                )
                parity = jnp.bitwise_xor(
                    bit_of(index_all, first_cut), bit_of(index_all, second_cut)
                )
                signs = (1 - 2 * parity).astype(jnp.float32)
                chosen = path_index[cut_number] == 0
                angle_now = cut_angle[cut_number]
                keep_part = jnp.where(chosen, jnp.cos(angle_now), jnp.zeros_like(angle_now))
                turn_part = jnp.where(chosen, jnp.zeros_like(angle_now), jnp.sin(angle_now))
                result = jnp.stack(
                    (
                        keep_part * result[0] + turn_part * signs * result[1],
                        keep_part * result[1] - turn_part * signs * result[0],
                    )
                )
    return result


def any_slice(amplitudes, gate_matrices, *rest):
    g = lax.axis_size("hi").bit_length() - 1
    local_bits = amplitudes.shape[1].bit_length() - 1
    late_layers = gate_matrices.shape[0] - g
    fits = 3 <= g <= local_bits - g - 7 and local_bits - g >= 11 and 0 < late_layers <= 3
    plan = one_exchange if fits else shards
    return plan(amplitudes, gate_matrices, *rest)


def solution(mesh):
    placed = (
        P(None, ("paths", "hi")),
        P(),
        P("paths", None, None),
        P("paths", None),
        P("paths", None),
        P("paths"),
        P("paths"),
    )
    return jax.shard_map(
        any_slice, mesh=mesh, in_specs=placed, out_specs=P(None, ("paths", "hi")), check_vma=False
    )
```

```python
import functools
import math

import jax
import jax.numpy as jnp
from jax import lax
from jax.experimental import pallas as pl
from jax.experimental.pallas import tpu as pltpu
from jax.sharding import PartitionSpec as P

LANES = 128
SUB = 8
MESH = pl.DeviceIdType.MESH


def quarter_sincos(turns):
    whole = jnp.floor(turns + 0.5)
    rest = turns - whole
    square = rest * rest
    half_pi = math.pi / 2
    sin_terms = [(-1) ** k * half_pi ** (2 * k + 1) / math.factorial(2 * k + 1) for k in range(5)]
    cos_terms = [(-1) ** k * half_pi ** (2 * k) / math.factorial(2 * k) for k in range(6)]
    sine = jnp.full_like(square, sin_terms[-1])
    for term in sin_terms[-2::-1]:
        sine = sine * square + term
    sine = sine * rest
    cosine = jnp.full_like(square, cos_terms[-1])
    for term in cos_terms[-2::-1]:
        cosine = cosine * square + term
    count = whole.astype(jnp.int32)
    odd = (count & 1) == 1
    sin_out = jnp.where(odd, cosine, sine)
    cos_out = jnp.where(odd, sine, cosine)
    sin_out = jnp.where((count & 2) == 2, -sin_out, sin_out)
    cos_out = jnp.where(((count + 1) & 2) == 2, -cos_out, cos_out)
    return sin_out, cos_out


def swap_half(value):
    return pltpu.roll(value, LANES // 2, axis=1)


def spread(value, moves):
    total = None
    for a, b in moves:
        term = ((value >> a) & 1) << b
        total = term if total is None else total + term
    return total


def circuit_kernel(
    g, local_bits, layers, pairs, cuts,
    amp_ref, gate_ref, qubit_in, angle_in, cut_qubit_in, cut_angle_in, path_in, out_ref,
    qubit_ref, angle_ref, cut_qubit_ref, cut_angle_ref, path_ref,
    recv, weights, gates, cos_all, sin_all, turned,
    send_sem, recv_sem, own_sem, gate_sem, small_sem,
):
    n = 2**g
    block_bits = local_bits - g - 7
    chunks = 2 ** (block_bits - 3)
    piece = 2 * SUB
    rows = n * SUB
    me = lax.axis_index("hi")
    order = sorted(range(1, n), key=lambda off: abs(off - n // 2))

    def block_rows(owner, chunk):
        return pl.ds(pl.multiple_of((owner * chunks + chunk) * piece, piece), piece)

    def slot_rows(source):
        return pl.ds(pl.multiple_of(source * piece, piece), piece)

    def remote(chunk, off):
        peer = lax.rem(me + off, n)
        return pltpu.make_async_remote_copy(
            src_ref=amp_ref.at[block_rows(peer, chunk)],
            dst_ref=recv.at[chunk, slot_rows(me)],
            send_sem=send_sem.at[chunk, off],
            recv_sem=recv_sem.at[chunk, off],
            device_id={"hi": peer},
            device_id_type=MESH,
        )

    def own(chunk):
        return pltpu.make_async_copy(
            amp_ref.at[block_rows(me, chunk)], recv.at[chunk, slot_rows(me)], own_sem.at[chunk]
        )

    gate_copy = pltpu.make_async_copy(gate_ref, gates, gate_sem)
    gate_copy.start()
    smalls = (
        (qubit_in, qubit_ref),
        (angle_in, angle_ref),
        (cut_qubit_in, cut_qubit_ref),
        (cut_angle_in, cut_angle_ref),
        (path_in, path_ref),
    )
    small_copies = [
        pltpu.make_async_copy(source, target, small_sem.at[k])
        for k, (source, target) in enumerate(smalls)
    ]
    for small_copy in small_copies:
        small_copy.start()

    barrier = pltpu.get_barrier_semaphore()
    for off in order:
        pl.semaphore_signal(
            barrier, inc=1, device_id={"hi": lax.rem(me + off, n)}, device_id_type=MESH
        )
    pl.semaphore_wait(barrier, n - 1)

    @pl.loop(0, chunks)
    def _(chunk):
        for off in order:
            remote(chunk, off).start()
        own(chunk).start()

    gate_copy.wait()
    low_lanes = lax.broadcasted_iota(jnp.int32, (64, LANES), 1) < 64

    @pl.loop(0, layers)
    def _(layer):
        real_t = gates[layer, 0].astype(jnp.float32).T
        imag_t = gates[layer, 1].astype(jnp.float32).T
        for t in range(2):
            real_rows = real_t[t * 64 : (t + 1) * 64]
            imag_rows = imag_t[t * 64 : (t + 1) * 64]
            real_turned, imag_turned = swap_half(real_rows), swap_half(imag_rows)
            parts = (
                (
                    jnp.where(low_lanes, real_rows, imag_turned),
                    jnp.where(low_lanes, real_turned, imag_rows),
                ),
                (
                    jnp.where(low_lanes, -imag_rows, real_turned),
                    jnp.where(low_lanes, -imag_turned, real_rows),
                ),
            )
            for c in range(2):
                for t_out in range(2):
                    weights[
                        layer,
                        t * 128 + c * 64 : t * 128 + c * 64 + 64,
                        t_out * 128 : t_out * 128 + 128,
                    ] = parts[c][t_out].astype(jnp.bfloat16)

    def chunk_row(k):
        return block_bits + 3 + k if 10 + k < 7 + g else 3 + k

    lane = lax.broadcasted_iota(jnp.int32, (n, SUB, LANES), 2)
    first = lax.broadcasted_iota(jnp.int32, (n, SUB, LANES), 0)
    second = lax.broadcasted_iota(jnp.int32, (n, SUB, LANES), 1)
    flat_low = lax.broadcasted_iota(jnp.int32, (rows, LANES), 1) < 64
    to_quarter = 2.0 / math.pi

    def entry_index(layer, chunk):
        def place(q):
            if 7 <= q <= 7 + layer:
                return q - 7 + local_bits
            if local_bits <= q <= local_bits + layer:
                return q - local_bits + 7
            return q

        scalar = spread(chunk, [(k, place(10 + k)) for k in range(block_bits - 3)]) + spread(
            me, [(k, place(local_bits - g + k)) for k in range(g)]
        )
        return (
            (lane + spread(second, [(k, place(7 + k)) for k in range(3)]) + scalar)
            + spread(first, [(k, place(local_bits + k)) for k in range(g)])
        )

    def final_index(chunk):
        low_part = lax.broadcasted_iota(jnp.int32, (SUB, n, LANES), 0)
        source = lax.broadcasted_iota(jnp.int32, (SUB, n, LANES), 1)
        lane_part = lax.broadcasted_iota(jnp.int32, (SUB, n, LANES), 2)
        scalar = spread(chunk, [(k, 7 + chunk_row(k)) for k in range(block_bits - 3)])
        return lane_part + (source << 7) + (low_part << (7 + block_bits)) + (
            scalar + (me << local_bits)
        )

    for small_copy in small_copies:
        small_copy.wait()
    cut_mask = jnp.int32(0)
    cut_turns = jnp.float32(0)
    cut_size = jnp.full((SUB, LANES), 1.0, jnp.float32)
    for k in range(cuts):
        kept = path_ref[k] == 0
        bits = (jnp.int32(1) << cut_qubit_ref[0, k]) ^ (jnp.int32(1) << cut_qubit_ref[1, k])
        cut_mask = cut_mask ^ jnp.where(kept, 0, bits)
        cut_turns = cut_turns - jnp.where(kept, 0.0, 1.0)
        sine, cosine = quarter_sincos(
            jnp.full((SUB, LANES), cut_angle_ref[k], jnp.float32) * to_quarter
        )
        kept_all = jnp.full((SUB, LANES), path_ref[k], jnp.int32) == 0
        cut_size = cut_size * jnp.where(kept_all, cosine, sine)

    for layer in range(layers):
        masks = []
        for k in range(pairs):
            mask = (jnp.int32(1) << qubit_ref[layer, 0, k]) | (
                jnp.int32(1) << qubit_ref[layer, 1, k]
            )
            masks.append((mask, angle_ref[layer, k] * to_quarter))

        @pl.loop(0, chunks)
        def _(chunk):
            index = entry_index(layer, chunk) if layer < g else final_index(chunk)
            index = index.reshape(rows, LANES)
            turns = jnp.zeros((rows, LANES), jnp.float32)
            for mask, angle in masks:
                turns = turns + jnp.where((index & mask) == mask, angle, 0.0)
            if layer == 0:
                folded = index & cut_mask
                for shift in (16, 8, 4, 2, 1):
                    folded = folded ^ (folded >> shift)
                turns = turns + cut_turns + ((folded & 1) * 2).astype(jnp.float32)
            sine, cosine = quarter_sincos(turns)
            if layer == 0:
                size = jnp.broadcast_to(cut_size[None], (n, SUB, LANES)).reshape(rows, LANES)
                sine, cosine = sine * size, cosine * size
            sine_turned, cosine_turned = swap_half(sine), swap_half(cosine)
            cos_all[layer, chunk, 0] = jnp.where(flat_low, cosine, cosine_turned)
            cos_all[layer, chunk, 1] = jnp.where(flat_low, cosine_turned, cosine)
            sin_all[layer, chunk, 0] = jnp.where(flat_low, -sine, sine_turned)
            sin_all[layer, chunk, 1] = jnp.where(flat_low, -sine_turned, sine)

    def layer_step(state, layer, chunk, outer, inner):
        shaped = state.reshape(2, outer, 2, inner, LANES)
        joined = jnp.concatenate(
            (shaped[:, :, 0].reshape(rows, LANES), shaped[:, :, 1].reshape(rows, LANES)), axis=1
        )
        high = joined.astype(jnp.bfloat16)
        rest = (joined - high.astype(jnp.float32)).astype(jnp.bfloat16)
        gate = weights[layer]
        product = jnp.dot(high, gate, preferred_element_type=jnp.float32) + jnp.dot(
            rest, gate, preferred_element_type=jnp.float32
        )
        back = jnp.stack(
            (
                product[:, :LANES].reshape(2, outer, inner, LANES),
                product[:, LANES:].reshape(2, outer, inner, LANES),
            ),
            axis=2,
        ).reshape(2 * rows, LANES)
        cosine = cos_all[layer, chunk].reshape(2 * rows, LANES)
        sine = sin_all[layer, chunk].reshape(2 * rows, LANES)
        return back * cosine + swap_half(back) * sine

    @pl.loop(0, chunks)
    def _(chunk):
        own(chunk).wait()
        for off in order:
            remote(chunk, off).wait_recv()
        real = recv[chunk, pl.ds(0, rows, stride=2), :]
        imag = recv[chunk, pl.ds(1, rows, stride=2), :]
        state = jnp.concatenate(
            (
                jnp.where(flat_low, real, swap_half(imag)),
                jnp.where(flat_low, swap_half(real), imag),
            ),
            axis=0,
        )
        for layer in range(g):
            state = layer_step(state, layer, chunk, 2 ** (g - 1 - layer), 2**layer * SUB)
        turned[...] = state
        state = jnp.concatenate(
            [
                turned[pl.ds(b * rows + low, n, stride=SUB), :]
                for b in range(2)
                for low in range(SUB)
            ],
            axis=0,
        )
        for layer in range(g, layers):
            k = layer - g
            state = layer_step(state, layer, chunk, 2 ** (2 - k), 2**k * n)
        zero, one = state[:rows], state[rows:]
        real = jnp.where(flat_low, zero, swap_half(one))
        imag = jnp.where(flat_low, swap_half(zero), one)
        base = spread(chunk, [(k, chunk_row(k)) for k in range(block_bits - 3)])
        for low in range(SUB):
            start = pl.multiple_of(2 * (base + (low << block_bits)), 2 * n)
            out_ref[pl.ds(start, n, stride=2), :] = real[low * n : (low + 1) * n]
            out_ref[pl.ds(start + 1, n, stride=2), :] = imag[low * n : (low + 1) * n]

    @pl.loop(0, chunks)
    def _(chunk):
        for off in order:
            remote(chunk, off).wait_send()


def one_exchange(
    amplitudes, gate_matrices, phase_qubits, phase_angles, cut_qubits, cut_angle, path_index
):
    g = lax.axis_size("hi").bit_length() - 1
    amp_count = amplitudes.shape[1]
    local_bits = amp_count.bit_length() - 1
    layers, pairs = phase_angles.shape
    cuts = cut_angle.shape[0]
    n = 2**g
    chunks = 2 ** (local_bits - g - 10)
    rows = n * SUB
    all_rows = amp_count // LANES
    whole = amplitudes.reshape(2, all_rows, LANES).transpose(1, 0, 2).reshape(2 * all_rows, LANES)
    hbm = pl.BlockSpec(memory_space=pltpu.HBM)
    result = pl.pallas_call(
        functools.partial(circuit_kernel, g, local_bits, layers, pairs, cuts),
        out_shape=pltpu.VMEM((2 * all_rows, LANES), jnp.float32),
        in_specs=[hbm] * 7,
        out_specs=pl.BlockSpec(memory_space=pltpu.VMEM),
        scratch_shapes=[
            pltpu.SMEM((layers, 2, pairs), jnp.int32),
            pltpu.SMEM(phase_angles.shape, jnp.float32),
            pltpu.SMEM((2, cuts), jnp.int32),
            pltpu.SMEM(cut_angle.shape, jnp.float32),
            pltpu.SMEM(path_index.shape, jnp.int32),
            pltpu.VMEM((chunks, 2 * rows, LANES), jnp.float32),
            pltpu.VMEM((layers, 256, 256), jnp.bfloat16),
            pltpu.VMEM(gate_matrices.shape, jnp.bfloat16),
            pltpu.VMEM((layers, chunks, 2, rows, LANES), jnp.float32),
            pltpu.VMEM((layers, chunks, 2, rows, LANES), jnp.float32),
            pltpu.VMEM((2 * rows, LANES), jnp.float32),
            pltpu.SemaphoreType.DMA((chunks, n)),
            pltpu.SemaphoreType.DMA((chunks, n)),
            pltpu.SemaphoreType.DMA((chunks,)),
            pltpu.SemaphoreType.DMA,
            pltpu.SemaphoreType.DMA((5,)),
        ],
        compiler_params=pltpu.CompilerParams(collective_id=0, has_side_effects=True),
    )(
        whole, gate_matrices, phase_qubits.transpose(0, 2, 1), phase_angles,
        cut_qubits.transpose(1, 0), cut_angle, path_index,
    )
    return result.reshape(all_rows, 2, LANES).transpose(1, 0, 2).reshape(2, amp_count)


def from_partner(value, axis, bit):
    return lax.ppermute(value, axis, [(i, i ^ 1 << bit) for i in range(lax.axis_size(axis))])


def real_form(matrix):
    real_part = matrix[0].astype(jnp.float32)
    imag_part = matrix[1].astype(jnp.float32)
    upper_rows = jnp.stack((real_part, -imag_part), axis=1)
    lower_rows = jnp.stack((imag_part, real_part), axis=1)
    stacked = jnp.stack((upper_rows, lower_rows), axis=0)
    return stacked.reshape(2, 2, 64, 2, 2, 64)


def apply_gate(amps_now, matrix, target, local_bits):
    shaped = amps_now.reshape(2, 2 ** (local_bits - 1 - target), 2, 2 ** (target - 7), 2, 64)
    result = jnp.einsum(
        "wxyzbd,zabced->waxcey", real_form(matrix), shaped, precision=lax.Precision.HIGHEST
    )
    return result.reshape(2, -1)


def rotate(amps_now, theta):
    cosine = jnp.cos(theta)
    sine = jnp.sin(theta)
    return jnp.stack(
        (cosine * amps_now[0] - sine * amps_now[1], sine * amps_now[0] + cosine * amps_now[1])
    )


def bit_of(index_all, qubit):
    return jnp.bitwise_and(jnp.right_shift(index_all, qubit), 1)


def located(qubit, first_open, global_count, local_bits):
    moved_up = (qubit >= 7 + first_open) & (qubit < 7 + global_count)
    moved_down = (qubit >= local_bits + first_open) & (qubit < local_bits + global_count)
    return jnp.where(
        moved_up, qubit - 7 + local_bits, jnp.where(moved_down, qubit - local_bits + 7, qubit)
    )


def enter_qubit(amps_now, bit_number, local_bits, device_place):
    shaped = amps_now.reshape(2, 2 ** (local_bits - 8 - bit_number), 2, 2**bit_number, 128)
    zero_half = shaped[:, :, 0]
    one_half = shaped[:, :, 1]
    upper_side = jnp.bitwise_and(jnp.right_shift(device_place, bit_number), 1) == 1
    kept_half = jnp.where(upper_side, one_half, zero_half)
    sent_half = jnp.where(upper_side, zero_half, one_half)
    came_half = from_partner(sent_half, "hi", bit_number)
    new_zero = jnp.where(upper_side, came_half, kept_half)
    new_one = jnp.where(upper_side, kept_half, came_half)
    return jnp.stack((new_zero, new_one), axis=2).reshape(2, -1)


def shards(
    amplitudes, gate_matrices, phase_qubits, phase_angles, cut_qubits, cut_angle, path_index
):
    global_count = lax.axis_size("hi").bit_length() - 1
    amp_count = amplitudes.shape[1]
    local_bits = amp_count.bit_length() - 1
    device_place = lax.axis_index("hi")
    index_all = device_place * amp_count + lax.iota(jnp.int32, amp_count)
    layer_count = gate_matrices.shape[0]
    result = amplitudes
    for layer_number in range(layer_count):
        if layer_number < global_count:
            result = enter_qubit(result, layer_number, local_bits, device_place)
            target = 7 + layer_number
        else:
            if layer_number == global_count:
                shaped = result.reshape(2, 2**global_count, 2 ** (local_bits - global_count))
                result = lax.all_to_all(
                    shaped, "hi", split_axis=1, concat_axis=1, tiled=True
                ).reshape(2, -1)
            target = local_bits - 2 * global_count + layer_number
        result = apply_gate(result, gate_matrices[layer_number], target, local_bits)
        theta = jnp.zeros((amp_count,), jnp.float32)
        for pair_number in range(phase_qubits.shape[1]):
            first_pos = located(
                phase_qubits[layer_number, pair_number, 0], global_count, global_count, local_bits
            )
            second_pos = located(
                phase_qubits[layer_number, pair_number, 1], global_count, global_count, local_bits
            )
            both_bits = bit_of(index_all, first_pos) * bit_of(index_all, second_pos)
            theta = theta + phase_angles[layer_number, pair_number] * both_bits.astype(jnp.float32)
        result = rotate(result, theta)
        if layer_number == 0:
            for cut_number in range(cut_qubits.shape[0]):
                first_cut = located(
                    cut_qubits[cut_number, 0], global_count, global_count, local_bits
                )
                second_cut = located(
                    cut_qubits[cut_number, 1], global_count, global_count, local_bits
                )
                parity = jnp.bitwise_xor(
                    bit_of(index_all, first_cut), bit_of(index_all, second_cut)
                )
                signs = (1 - 2 * parity).astype(jnp.float32)
                chosen = path_index[cut_number] == 0
                angle_now = cut_angle[cut_number]
                keep_part = jnp.where(chosen, jnp.cos(angle_now), jnp.zeros_like(angle_now))
                turn_part = jnp.where(chosen, jnp.zeros_like(angle_now), jnp.sin(angle_now))
                result = jnp.stack(
                    (
                        keep_part * result[0] + turn_part * signs * result[1],
                        keep_part * result[1] - turn_part * signs * result[0],
                    )
                )
    return result


def any_slice(amplitudes, gate_matrices, *rest):
    g = lax.axis_size("hi").bit_length() - 1
    local_bits = amplitudes.shape[1].bit_length() - 1
    late_layers = gate_matrices.shape[0] - g
    fits = 3 <= g <= local_bits - g - 7 and local_bits - g >= 11 and 0 < late_layers <= 3
    plan = one_exchange if fits else shards
    return plan(amplitudes, gate_matrices, *rest)


def solution(mesh):
    placed = (
        P(None, ("paths", "hi")),
        P(),
        P("paths", None, None),
        P("paths", None),
        P("paths", None),
        P("paths"),
        P("paths"),
    )
    return jax.shard_map(
        any_slice, mesh=mesh, in_specs=placed, out_specs=P(None, ("paths", "hi")), check_vma=False
    )
```

```python
import functools
import math

import jax
import jax.numpy as jnp
from jax import lax
from jax.experimental import pallas as pl
from jax.experimental.pallas import tpu as pltpu
from jax.sharding import PartitionSpec as P

LANES = 128
SUB = 8
MESH = pl.DeviceIdType.MESH


def quarter_sincos(turns):
    whole = jnp.floor(turns + 0.5)
    rest = turns - whole
    square = rest * rest
    half_pi = math.pi / 2
    sin_terms = [(-1) ** k * half_pi ** (2 * k + 1) / math.factorial(2 * k + 1) for k in range(5)]
    cos_terms = [(-1) ** k * half_pi ** (2 * k) / math.factorial(2 * k) for k in range(6)]
    sine = jnp.full_like(square, sin_terms[-1])
    for term in sin_terms[-2::-1]:
        sine = sine * square + term
    sine = sine * rest
    cosine = jnp.full_like(square, cos_terms[-1])
    for term in cos_terms[-2::-1]:
        cosine = cosine * square + term
    count = whole.astype(jnp.int32)
    odd = (count & 1) == 1
    sin_out = jnp.where(odd, cosine, sine)
    cos_out = jnp.where(odd, sine, cosine)
    sin_out = jnp.where((count & 2) == 2, -sin_out, sin_out)
    cos_out = jnp.where(((count + 1) & 2) == 2, -cos_out, cos_out)
    return sin_out, cos_out


def swap_half(value):
    return pltpu.roll(value, LANES // 2, axis=1)


def spread(value, moves):
    total = None
    for a, b in moves:
        term = ((value >> a) & 1) << b
        total = term if total is None else total + term
    return total


def circuit_kernel(
    g, local_bits, layers, pairs, cuts,
    amp_ref, gate_ref, qubit_in, angle_in, cut_qubit_in, cut_angle_in, path_in, out_ref,
    qubit_ref, angle_ref, cut_qubit_ref, cut_angle_ref, path_ref,
    recv, weights, gates, cos_all, sin_all, turned,
    send_sem, recv_sem, own_sem, gate_sem, small_sem,
):
    n = 2**g
    block_bits = local_bits - g - 7
    chunks = 2 ** (block_bits - 3)
    piece = 2 * SUB
    rows = n * SUB
    me = lax.axis_index("hi")
    order = range(1, n)

    def block_rows(owner, chunk):
        return pl.ds(pl.multiple_of((owner * chunks + chunk) * piece, piece), piece)

    def slot_rows(source):
        return pl.ds(pl.multiple_of(source * piece, piece), piece)

    def remote(chunk, off):
        peer = lax.rem(me + off, n)
        return pltpu.make_async_remote_copy(
            src_ref=amp_ref.at[block_rows(peer, chunk)],
            dst_ref=recv.at[chunk, slot_rows(me)],
            send_sem=send_sem.at[chunk, off],
            recv_sem=recv_sem.at[chunk, off],
            device_id={"hi": peer},
            device_id_type=MESH,
        )

    def own(chunk):
        return pltpu.make_async_copy(
            amp_ref.at[block_rows(me, chunk)], recv.at[chunk, slot_rows(me)], own_sem.at[chunk]
        )

    gate_copy = pltpu.make_async_copy(gate_ref, gates, gate_sem)
    gate_copy.start()
    smalls = (
        (qubit_in, qubit_ref),
        (angle_in, angle_ref),
        (cut_qubit_in, cut_qubit_ref),
        (cut_angle_in, cut_angle_ref),
        (path_in, path_ref),
    )
    small_copies = [
        pltpu.make_async_copy(source, target, small_sem.at[k])
        for k, (source, target) in enumerate(smalls)
    ]
    for small_copy in small_copies:
        small_copy.start()

    barrier = pltpu.get_barrier_semaphore()
    for off in order:
        pl.semaphore_signal(
            barrier, inc=1, device_id={"hi": lax.rem(me + off, n)}, device_id_type=MESH
        )
    pl.semaphore_wait(barrier, n - 1)

    @pl.loop(0, chunks)
    def _(chunk):
        for off in order:
            remote(chunk, off).start()
        own(chunk).start()

    gate_copy.wait()
    low_lanes = lax.broadcasted_iota(jnp.int32, (64, LANES), 1) < 64

    @pl.loop(0, layers)
    def _(layer):
        real_t = gates[layer, 0].astype(jnp.float32).T
        imag_t = gates[layer, 1].astype(jnp.float32).T
        for t in range(2):
            real_rows = real_t[t * 64 : (t + 1) * 64]
            imag_rows = imag_t[t * 64 : (t + 1) * 64]
            real_turned, imag_turned = swap_half(real_rows), swap_half(imag_rows)
            parts = (
                (
                    jnp.where(low_lanes, real_rows, imag_turned),
                    jnp.where(low_lanes, real_turned, imag_rows),
                ),
                (
                    jnp.where(low_lanes, -imag_rows, real_turned),
                    jnp.where(low_lanes, -imag_turned, real_rows),
                ),
            )
            for c in range(2):
                for t_out in range(2):
                    weights[
                        layer,
                        t * 128 + c * 64 : t * 128 + c * 64 + 64,
                        t_out * 128 : t_out * 128 + 128,
                    ] = parts[c][t_out].astype(jnp.bfloat16)

    def chunk_row(k):
        return block_bits + 3 + k if 10 + k < 7 + g else 3 + k

    lane = lax.broadcasted_iota(jnp.int32, (n, SUB, LANES), 2)
    first = lax.broadcasted_iota(jnp.int32, (n, SUB, LANES), 0)
    second = lax.broadcasted_iota(jnp.int32, (n, SUB, LANES), 1)
    flat_low = lax.broadcasted_iota(jnp.int32, (rows, LANES), 1) < 64
    to_quarter = 2.0 / math.pi

    def entry_index(layer, chunk):
        def place(q):
            if 7 <= q <= 7 + layer:
                return q - 7 + local_bits
            if local_bits <= q <= local_bits + layer:
                return q - local_bits + 7
            return q

        scalar = spread(chunk, [(k, place(10 + k)) for k in range(block_bits - 3)]) + spread(
            me, [(k, place(local_bits - g + k)) for k in range(g)]
        )
        return (
            (lane + spread(second, [(k, place(7 + k)) for k in range(3)]) + scalar)
            + spread(first, [(k, place(local_bits + k)) for k in range(g)])
        )

    def final_index(chunk):
        low_part = lax.broadcasted_iota(jnp.int32, (SUB, n, LANES), 0)
        source = lax.broadcasted_iota(jnp.int32, (SUB, n, LANES), 1)
        lane_part = lax.broadcasted_iota(jnp.int32, (SUB, n, LANES), 2)
        scalar = spread(chunk, [(k, 7 + chunk_row(k)) for k in range(block_bits - 3)])
        return lane_part + (source << 7) + (low_part << (7 + block_bits)) + (
            scalar + (me << local_bits)
        )

    for small_copy in small_copies:
        small_copy.wait()
    cut_mask = jnp.int32(0)
    cut_turns = jnp.float32(0)
    cut_size = jnp.full((SUB, LANES), 1.0, jnp.float32)
    for k in range(cuts):
        kept = path_ref[k] == 0
        bits = (jnp.int32(1) << cut_qubit_ref[0, k]) ^ (jnp.int32(1) << cut_qubit_ref[1, k])
        cut_mask = cut_mask ^ jnp.where(kept, 0, bits)
        cut_turns = cut_turns - jnp.where(kept, 0.0, 1.0)
        sine, cosine = quarter_sincos(
            jnp.full((SUB, LANES), cut_angle_ref[k], jnp.float32) * to_quarter
        )
        kept_all = jnp.full((SUB, LANES), path_ref[k], jnp.int32) == 0
        cut_size = cut_size * jnp.where(kept_all, cosine, sine)

    for layer in range(layers):
        masks = []
        for k in range(pairs):
            mask = (jnp.int32(1) << qubit_ref[layer, 0, k]) | (
                jnp.int32(1) << qubit_ref[layer, 1, k]
            )
            masks.append((mask, angle_ref[layer, k] * to_quarter))

        @pl.loop(0, chunks)
        def _(chunk):
            index = entry_index(layer, chunk) if layer < g else final_index(chunk)
            index = index.reshape(rows, LANES)
            turns = jnp.zeros((rows, LANES), jnp.float32)
            for mask, angle in masks:
                turns = turns + jnp.where((index & mask) == mask, angle, 0.0)
            if layer == 0:
                folded = index & cut_mask
                for shift in (16, 8, 4, 2, 1):
                    folded = folded ^ (folded >> shift)
                turns = turns + cut_turns + ((folded & 1) * 2).astype(jnp.float32)
            sine, cosine = quarter_sincos(turns)
            if layer == 0:
                size = jnp.broadcast_to(cut_size[None], (n, SUB, LANES)).reshape(rows, LANES)
                sine, cosine = sine * size, cosine * size
            sine_turned, cosine_turned = swap_half(sine), swap_half(cosine)
            cos_all[layer, chunk, 0] = jnp.where(flat_low, cosine, cosine_turned)
            cos_all[layer, chunk, 1] = jnp.where(flat_low, cosine_turned, cosine)
            sin_all[layer, chunk, 0] = jnp.where(flat_low, -sine, sine_turned)
            sin_all[layer, chunk, 1] = jnp.where(flat_low, -sine_turned, sine)

    def layer_step(state, layer, chunk, outer, inner):
        shaped = state.reshape(2, outer, 2, inner, LANES)
        joined = jnp.concatenate(
            (shaped[:, :, 0].reshape(rows, LANES), shaped[:, :, 1].reshape(rows, LANES)), axis=1
        )
        high = joined.astype(jnp.bfloat16)
        rest = (joined - high.astype(jnp.float32)).astype(jnp.bfloat16)
        gate = weights[layer]
        both = jnp.dot(
            jnp.concatenate((high, rest), axis=0), gate, preferred_element_type=jnp.float32
        )
        product = both[:rows] + both[rows:]
        back = jnp.stack(
            (
                product[:, :LANES].reshape(2, outer, inner, LANES),
                product[:, LANES:].reshape(2, outer, inner, LANES),
            ),
            axis=2,
        ).reshape(2 * rows, LANES)
        cosine = cos_all[layer, chunk].reshape(2 * rows, LANES)
        sine = sin_all[layer, chunk].reshape(2 * rows, LANES)
        return back * cosine + swap_half(back) * sine

    @pl.loop(0, chunks)
    def _(chunk):
        own(chunk).wait()
        for off in order:
            remote(chunk, off).wait_recv()
        real = recv[chunk, pl.ds(0, rows, stride=2), :]
        imag = recv[chunk, pl.ds(1, rows, stride=2), :]
        state = jnp.concatenate(
            (
                jnp.where(flat_low, real, swap_half(imag)),
                jnp.where(flat_low, swap_half(real), imag),
            ),
            axis=0,
        )
        for layer in range(g):
            state = layer_step(state, layer, chunk, 2 ** (g - 1 - layer), 2**layer * SUB)
        turned[...] = state
        state = jnp.concatenate(
            [
                turned[pl.ds(b * rows + low, n, stride=SUB), :]
                for b in range(2)
                for low in range(SUB)
            ],
            axis=0,
        )
        for layer in range(g, layers):
            k = layer - g
            state = layer_step(state, layer, chunk, 2 ** (2 - k), 2**k * n)
        zero, one = state[:rows], state[rows:]
        real = jnp.where(flat_low, zero, swap_half(one))
        imag = jnp.where(flat_low, swap_half(zero), one)
        base = spread(chunk, [(k, chunk_row(k)) for k in range(block_bits - 3)])
        for low in range(SUB):
            start = pl.multiple_of(2 * (base + (low << block_bits)), 2 * n)
            out_ref[pl.ds(start, n, stride=2), :] = real[low * n : (low + 1) * n]
            out_ref[pl.ds(start + 1, n, stride=2), :] = imag[low * n : (low + 1) * n]

    @pl.loop(0, chunks)
    def _(chunk):
        for off in order:
            remote(chunk, off).wait_send()


def one_exchange(
    amplitudes, gate_matrices, phase_qubits, phase_angles, cut_qubits, cut_angle, path_index
):
    g = lax.axis_size("hi").bit_length() - 1
    amp_count = amplitudes.shape[1]
    local_bits = amp_count.bit_length() - 1
    layers, pairs = phase_angles.shape
    cuts = cut_angle.shape[0]
    n = 2**g
    chunks = 2 ** (local_bits - g - 10)
    rows = n * SUB
    all_rows = amp_count // LANES
    whole = amplitudes.reshape(2, all_rows, LANES).transpose(1, 0, 2).reshape(2 * all_rows, LANES)
    hbm = pl.BlockSpec(memory_space=pltpu.HBM)
    result = pl.pallas_call(
        functools.partial(circuit_kernel, g, local_bits, layers, pairs, cuts),
        out_shape=pltpu.VMEM((2 * all_rows, LANES), jnp.float32),
        in_specs=[hbm] * 7,
        out_specs=pl.BlockSpec(memory_space=pltpu.VMEM),
        scratch_shapes=[
            pltpu.SMEM((layers, 2, pairs), jnp.int32),
            pltpu.SMEM(phase_angles.shape, jnp.float32),
            pltpu.SMEM((2, cuts), jnp.int32),
            pltpu.SMEM(cut_angle.shape, jnp.float32),
            pltpu.SMEM(path_index.shape, jnp.int32),
            pltpu.VMEM((chunks, 2 * rows, LANES), jnp.float32),
            pltpu.VMEM((layers, 256, 256), jnp.bfloat16),
            pltpu.VMEM(gate_matrices.shape, jnp.bfloat16),
            pltpu.VMEM((layers, chunks, 2, rows, LANES), jnp.float32),
            pltpu.VMEM((layers, chunks, 2, rows, LANES), jnp.float32),
            pltpu.VMEM((2 * rows, LANES), jnp.float32),
            pltpu.SemaphoreType.DMA((chunks, n)),
            pltpu.SemaphoreType.DMA((chunks, n)),
            pltpu.SemaphoreType.DMA((chunks,)),
            pltpu.SemaphoreType.DMA,
            pltpu.SemaphoreType.DMA((5,)),
        ],
        compiler_params=pltpu.CompilerParams(collective_id=0, has_side_effects=True),
    )(
        whole, gate_matrices, phase_qubits.transpose(0, 2, 1), phase_angles,
        cut_qubits.transpose(1, 0), cut_angle, path_index,
    )
    return result.reshape(all_rows, 2, LANES).transpose(1, 0, 2).reshape(2, amp_count)


def from_partner(value, axis, bit):
    return lax.ppermute(value, axis, [(i, i ^ 1 << bit) for i in range(lax.axis_size(axis))])


def real_form(matrix):
    real_part = matrix[0].astype(jnp.float32)
    imag_part = matrix[1].astype(jnp.float32)
    upper_rows = jnp.stack((real_part, -imag_part), axis=1)
    lower_rows = jnp.stack((imag_part, real_part), axis=1)
    stacked = jnp.stack((upper_rows, lower_rows), axis=0)
    return stacked.reshape(2, 2, 64, 2, 2, 64)


def apply_gate(amps_now, matrix, target, local_bits):
    shaped = amps_now.reshape(2, 2 ** (local_bits - 1 - target), 2, 2 ** (target - 7), 2, 64)
    result = jnp.einsum(
        "wxyzbd,zabced->waxcey", real_form(matrix), shaped, precision=lax.Precision.HIGHEST
    )
    return result.reshape(2, -1)


def rotate(amps_now, theta):
    cosine = jnp.cos(theta)
    sine = jnp.sin(theta)
    return jnp.stack(
        (cosine * amps_now[0] - sine * amps_now[1], sine * amps_now[0] + cosine * amps_now[1])
    )


def bit_of(index_all, qubit):
    return jnp.bitwise_and(jnp.right_shift(index_all, qubit), 1)


def located(qubit, first_open, global_count, local_bits):
    moved_up = (qubit >= 7 + first_open) & (qubit < 7 + global_count)
    moved_down = (qubit >= local_bits + first_open) & (qubit < local_bits + global_count)
    return jnp.where(
        moved_up, qubit - 7 + local_bits, jnp.where(moved_down, qubit - local_bits + 7, qubit)
    )


def enter_qubit(amps_now, bit_number, local_bits, device_place):
    shaped = amps_now.reshape(2, 2 ** (local_bits - 8 - bit_number), 2, 2**bit_number, 128)
    zero_half = shaped[:, :, 0]
    one_half = shaped[:, :, 1]
    upper_side = jnp.bitwise_and(jnp.right_shift(device_place, bit_number), 1) == 1
    kept_half = jnp.where(upper_side, one_half, zero_half)
    sent_half = jnp.where(upper_side, zero_half, one_half)
    came_half = from_partner(sent_half, "hi", bit_number)
    new_zero = jnp.where(upper_side, came_half, kept_half)
    new_one = jnp.where(upper_side, kept_half, came_half)
    return jnp.stack((new_zero, new_one), axis=2).reshape(2, -1)


def shards(
    amplitudes, gate_matrices, phase_qubits, phase_angles, cut_qubits, cut_angle, path_index
):
    global_count = lax.axis_size("hi").bit_length() - 1
    amp_count = amplitudes.shape[1]
    local_bits = amp_count.bit_length() - 1
    device_place = lax.axis_index("hi")
    index_all = device_place * amp_count + lax.iota(jnp.int32, amp_count)
    layer_count = gate_matrices.shape[0]
    result = amplitudes
    for layer_number in range(layer_count):
        if layer_number < global_count:
            result = enter_qubit(result, layer_number, local_bits, device_place)
            target = 7 + layer_number
        else:
            if layer_number == global_count:
                shaped = result.reshape(2, 2**global_count, 2 ** (local_bits - global_count))
                result = lax.all_to_all(
                    shaped, "hi", split_axis=1, concat_axis=1, tiled=True
                ).reshape(2, -1)
            target = local_bits - 2 * global_count + layer_number
        result = apply_gate(result, gate_matrices[layer_number], target, local_bits)
        theta = jnp.zeros((amp_count,), jnp.float32)
        for pair_number in range(phase_qubits.shape[1]):
            first_pos = located(
                phase_qubits[layer_number, pair_number, 0], global_count, global_count, local_bits
            )
            second_pos = located(
                phase_qubits[layer_number, pair_number, 1], global_count, global_count, local_bits
            )
            both_bits = bit_of(index_all, first_pos) * bit_of(index_all, second_pos)
            theta = theta + phase_angles[layer_number, pair_number] * both_bits.astype(jnp.float32)
        result = rotate(result, theta)
        if layer_number == 0:
            for cut_number in range(cut_qubits.shape[0]):
                first_cut = located(
                    cut_qubits[cut_number, 0], global_count, global_count, local_bits
                )
                second_cut = located(
                    cut_qubits[cut_number, 1], global_count, global_count, local_bits
                )
                parity = jnp.bitwise_xor(
                    bit_of(index_all, first_cut), bit_of(index_all, second_cut)
                )
                signs = (1 - 2 * parity).astype(jnp.float32)
                chosen = path_index[cut_number] == 0
                angle_now = cut_angle[cut_number]
                keep_part = jnp.where(chosen, jnp.cos(angle_now), jnp.zeros_like(angle_now))
                turn_part = jnp.where(chosen, jnp.zeros_like(angle_now), jnp.sin(angle_now))
                result = jnp.stack(
                    (
                        keep_part * result[0] + turn_part * signs * result[1],
                        keep_part * result[1] - turn_part * signs * result[0],
                    )
                )
    return result


def any_slice(amplitudes, gate_matrices, *rest):
    g = lax.axis_size("hi").bit_length() - 1
    local_bits = amplitudes.shape[1].bit_length() - 1
    late_layers = gate_matrices.shape[0] - g
    fits = 3 <= g <= local_bits - g - 7 and local_bits - g >= 11 and 0 < late_layers <= 3
    plan = one_exchange if fits else shards
    return plan(amplitudes, gate_matrices, *rest)


def solution(mesh):
    placed = (
        P(None, ("paths", "hi")),
        P(),
        P("paths", None, None),
        P("paths", None),
        P("paths", None),
        P("paths"),
        P("paths"),
    )
    return jax.shard_map(
        any_slice, mesh=mesh, in_specs=placed, out_specs=P(None, ("paths", "hi")), check_vma=False
    )
```
